32 devices in a mesh: gx: 2 (over y), gy: 4 (over z), gz: 4 (over x, core).
Axes of the slice: x: 2, y: 2, z: 4, core: 2. Of those that a mesh axis runs over, the one named last changes fastest.
Arguments:
- couplings: float32 [18, 16, 32, 512], P(None, 'gx', 'gy', 'gz'), may hold values from 0.05 to 2
- diagonal: float32 [3, 16, 32, 512], P(None, 'gx', 'gy', 'gz'), may hold values from 0.01 to 0.1
- right_side: float32 [3, 16, 32, 512], P(None, 'gx', 'gy', 'gz'), may hold values from -6 to 6
- guess: float32 [3, 16, 32, 512], P(None, 'gx', 'gy', 'gz'), may hold values from -4 to 4
Outputs:
- solution: float32 [3, 16, 32, 512], P(None, 'gx', 'gy', 'gz')
The draws below stay inside these ranges and needn't reach their ends.
All inputs are finite; a program needn't handle non-finite values.
Results may differ from the reference program's by a relative error of at most 0.00011.
Values sent between devices are 32-bit elements; how exact they have to be, the bound alone decides.
A program may use at most 128 MiB of HBM per device.

```python
import math
import jax
import jax.numpy as jnp

LEVELS = 4
SWEEPS = 2
COARSE_SWEEPS = 8
NX = 16
NY = 32
NZ = 512


def smooth_field(base_key, number):
    field_key = jax.random.fold_in(base_key, number)
    freq_key, angle_key, sign_key = jax.random.split(field_key, 3)
    freqs = jax.random.uniform(freq_key, (3, 3), jnp.float32, 0.5, 2.0)
    signs = jnp.where(jax.random.bernoulli(sign_key, 0.5, (3, 3)), 1.0, -1.0).astype(jnp.float32)
    freqs = freqs * signs
    angles = jax.random.uniform(angle_key, (3,), jnp.float32, 0.0, 2.0 * math.pi)
    coord_x = (jnp.arange(NX, dtype=jnp.float32) + 0.5) / NX
    coord_y = (jnp.arange(NY, dtype=jnp.float32) + 0.5) / NY
    coord_z = (jnp.arange(NZ, dtype=jnp.float32) + 0.5) / NZ
    result = jnp.zeros((NX, NY, NZ), jnp.float32)
    for wave in range(3):
        argument = freqs[wave, 0] * coord_x[:, None, None] + freqs[wave, 1] * coord_y[None, :, None] + freqs[wave, 2] * coord_z[None, None, :]
        result = result + jnp.cos(2.0 * math.pi * argument + angles[wave])
    return result / math.sqrt(1.5)


def draw_couplings(key, part):
    field_key = jax.random.fold_in(key, 1101)
    rough_key = jax.random.fold_in(key, 1102)
    sharpness = 3.0
    low_log = math.log(0.05)
    span_log = math.log(2.0) - math.log(0.05)
    planes = []
    for equation in range(3):
        fields = jnp.stack([smooth_field(field_key, 3 * equation + axis_number) for axis_number in range(3)])
        shares = jax.nn.softmax(sharpness * fields, axis=0)
        for axis_number in range(3):
            for side in range(2):
                uniform_part = jax.random.uniform(jax.random.fold_in(rough_key, 6 * equation + 2 * axis_number + side), (NX, NY, NZ), jnp.float32, 0.0, 1.0)
                exponent = 0.76 * shares[axis_number] + 0.24 * uniform_part
                planes.append(jnp.exp(low_log + span_log * exponent))
    return jnp.stack(planes).astype(jnp.float32)


def draw_diagonal(key, part):
    field_key = jax.random.fold_in(key, 2201)
    rough_key = jax.random.fold_in(key, 2202)
    power = 3.0
    planes = []
    for equation in range(3):
        region = jax.nn.sigmoid(2.0 * smooth_field(field_key, equation)) ** power
        uniform_part = jax.random.uniform(jax.random.fold_in(rough_key, equation), (NX, NY, NZ), jnp.float32, 0.0, 1.0)
        exponent = 0.68 * region + 0.32 * uniform_part
        planes.append(0.01 * jnp.exp(math.log(10.0) * exponent))
    return jnp.stack(planes).astype(jnp.float32)


def shard_levels(stream_key, shape, cuts, low, top_value):
    level = 1.0
    for dim, parts in cuts:
        steps = jax.random.uniform(jax.random.fold_in(jax.random.fold_in(stream_key, 6), dim), (parts,), jnp.float32, low / len(cuts), top_value / len(cuts))
        level = level * jnp.repeat(jnp.exp(steps), shape[dim] // parts).reshape((-1,) + (1,) * (len(shape) - 1 - dim))
    return level


def normal_values(key, shape, deviation, most, shards=(), held_as=jnp.bfloat16):
    gain = shard_levels(key, shape, shards, -0.22, 0.18) if shards else 1.0
    values = jax.random.normal(key, shape, jnp.float32) * deviation * gain
    return jnp.minimum(jnp.maximum(values, -most), most).astype(held_as)


def setup_inputs(seed: int = 0) -> dict:
    streams_of = jax.random.split(jax.random.key(seed), 5)
    couplings = draw_couplings(jax.random.fold_in(streams_of[4], 71), 0)
    diagonal = draw_diagonal(jax.random.fold_in(streams_of[4], 71), 0)
    right_side = normal_values(streams_of[2], (3, NX, NY, NZ), 1.0, 6.0, ((1, 2), (2, 4), (3, 4)), jnp.float32)
    guess = normal_values(streams_of[3], (3, NX, NY, NZ), 0.5, 4.0, ((1, 2), (2, 4), (3, 4)), jnp.float32)
    return {"couplings": couplings, "diagonal": diagonal, "right_side": right_side, "guess": guess}


damping = 0.8


def pad_zero(field):
    return jnp.pad(field, ((0, 0), (1, 1), (1, 1), (1, 1)))


def operate(field, padded, weights, total):
    near = [padded[:, 2:, 1:-1, 1:-1], padded[:, :-2, 1:-1, 1:-1],
            padded[:, 1:-1, 2:, 1:-1], padded[:, 1:-1, :-2, 1:-1],
            padded[:, 1:-1, 1:-1, 2:], padded[:, 1:-1, 1:-1, :-2]]
    offdiag = weights[:, 0] * near[0]
    for index in range(1, 6):
        offdiag = offdiag + weights[:, index] * near[index]
    return total * field - offdiag


def coarsen(array):
    shape = array.shape
    count = len(shape)
    blocks = array.reshape(shape[:-3] + (shape[-3] // 2, 2, shape[-2] // 2, 2, shape[-1] // 2, 2))
    return jnp.mean(blocks, axis=(count - 2, count, count + 2))


def refine(array):
    return jnp.repeat(jnp.repeat(jnp.repeat(array, 2, axis=-3), 2, axis=-2), 2, axis=-1)


def hierarchy(couplings, diagonal):
    weights = couplings.reshape((3, 6) + diagonal.shape[1:])
    local_diag = diagonal
    result = []
    for level in range(LEVELS):
        if level > 0:
            weights = coarsen(weights) * 0.25
            local_diag = coarsen(local_diag)
        result.append((weights, local_diag + jnp.sum(weights, axis=1)))
    return result


def reference(couplings, diagonal, right_side, guess):
    levels = hierarchy(couplings, diagonal)

    def cycle(level, field, rhs):
        weights, total = levels[level]

        def sweep(value):
            return value + damping * (rhs - operate(value, pad_zero(value), weights, total)) / total

        if level == LEVELS - 1:
            for step in range(COARSE_SWEEPS):
                field = sweep(field)
            return field
        for step in range(SWEEPS):
            field = sweep(field)
        resid = rhs - operate(field, pad_zero(field), weights, total)
        coarse_rhs = coarsen(resid)
        correction = cycle(level + 1, jnp.zeros_like(coarse_rhs), coarse_rhs)
        field = field + refine(correction)
        for step in range(SWEEPS):
            field = sweep(field)
        return field

    return cycle(0, guess, right_side)
```

```python
import functools

import jax
import jax.numpy as jnp
from jax import lax
from jax.experimental import pallas as pl
from jax.experimental.pallas import tpu as pltpu
from jax.sharding import PartitionSpec as P

SWEEPS = 2
COARSE_SWEEPS = 8
DAMP = 0.8
EQ = 3
MESH = pl.DeviceIdType.MESH
HIGH = lax.Precision.HIGHEST


def roll(value, shift, axis):
    size = value.shape[axis]
    shift = shift % size
    return value if shift == 0 else pltpu.roll(value, shift, axis)


def iota(shape, axis):
    return lax.broadcasted_iota(jnp.int32, shape, axis)


def kernel(
    dims, cores, w_ref, d_ref, b_ref, g_ref, out_ref,
    field, halo_x, halo_y, pack_s, pack_r, tot0, c0, w1, tot1, c1, b1,
    wsend, wall, bsend, ball, e2,
    s_sem, r_sem, ws_sem, wr_sem, bs_sem, br_sem, l_sem,
):
    ngx, ngy, ngz = dims
    nx, ny, nz = g_ref.shape[1:]
    qx, qy, qz = nx // 4, ny // 4, nz // 4
    rows = ngx * ngy
    nX = ngz // cores
    gx, gy, gz = lax.axis_index("gx"), lax.axis_index("gy"), lax.axis_index("gz")
    X, core = gz // cores, gz % cores
    row = gx * ngy + gy
    axes = (("gx", gx, ngx), ("gy", gy, ngy), ("gz", gz, ngz))

    def device(name, index):
        here = {"gx": gx, "gy": gy, "gz": gz}
        here[name] = index
        return (here["gx"], here["gy"], here["gz"])

    barrier = pltpu.get_barrier_semaphore()
    for name, index, count in axes:
        for step in range(1, count):
            pl.semaphore_signal(
                barrier, inc=1, device_id=device(name, (index + step) % count), device_id_type=MESH
            )

    rounds = field.shape[0]
    for name, index, count in axes:
        for side in range(2):
            @pl.when(index == (0 if side == 0 else count - 1))
            def _():
                for r in range(rounds):
                    if name == "gx":
                        halo_x[r, side] = jnp.zeros(halo_x.shape[2:], jnp.float32)
                    elif name == "gy":
                        lo = 0 if side == 0 else ny // 2
                        halo_y[r, :, :, lo : lo + ny // 2] = jnp.zeros(
                            (EQ, nx, ny // 2, nz), jnp.float32
                        )
                    else:
                        pack_r[r, side] = jnp.zeros(pack_r.shape[2:], jnp.float32)

    pl.semaphore_wait(barrier, ngx + ngy + ngz - 3)

    lane2 = iota((ny, nz), 1)

    def copies(r, n, s):
        src = g_ref if r == 0 else field.at[r]
        made = []
        for side in range(2):
            other = 1 - side
            for place, (name, index, count) in enumerate(axes):
                if name == "gx":
                    a = src.at[:, 0 if side == 0 else n - 1]
                    z = halo_x.at[r, other]
                elif name == "gy":
                    a = src.at[:, 0:n, pl.ds(0 if side == 0 else ny - s, s)]
                    z = halo_y.at[r, :, 0:n, pl.ds(ny - s if side == 0 else 0, s)]
                else:
                    a = pack_s.at[r, side]
                    z = pack_r.at[r, other]
                target = index - 1 if side == 0 else index + 1
                has_target = index > 0 if side == 0 else index < count - 1
                has_source = index < count - 1 if side == 0 else index > 0
                slot = 2 * place + side
                made.append((
                    pltpu.make_async_remote_copy(
                        src_ref=a, dst_ref=z,
                        send_sem=s_sem.at[r, slot], recv_sem=r_sem.at[r, slot],
                        device_id=device(name, jnp.clip(target, 0, count - 1)),
                        device_id_type=MESH,
                    ),
                    has_target, has_source,
                ))
        return made

    def send(r, value, n, s):
        low = jnp.zeros((ny, nz), jnp.float32)
        high = jnp.zeros((ny, nz), jnp.float32)
        for e in range(EQ):
            if r > 0:
                field[r, e, 0:n] = value[e]
            for i in range(n):
                here = lane2 == e * n + i
                low = jnp.where(here, jnp.broadcast_to(value[e][i, :, 0:1], (ny, nz)), low)
                high = jnp.where(here, jnp.broadcast_to(value[e][i, :, nz - 1 : nz], (ny, nz)), high)
        pack_s[r, 0] = low
        pack_s[r, 1] = high
        for copy, has_target, _ in copies(r, n, s):
            @pl.when(has_target)
            def _():
                copy.start()

    def receive(r, n, s):
        for copy, _, has_source in copies(r, n, s):
            @pl.when(has_source)
            def _():
                copy.wait_recv()

    def near_sum(r, value, e, n, s, weight):
        v = value[e]
        shape = (n, ny, nz)
        y, z = iota(shape, 1), iota(shape, 2)
        hy = halo_y[r, e, 0:n]
        low = pack_r[r, 0]
        high = pack_r[r, 1]
        zl = jnp.stack([jnp.broadcast_to(low[:, e * n + i : e * n + i + 1], (ny, nz)) for i in range(n)])
        zh = jnp.stack([jnp.broadcast_to(high[:, e * n + i : e * n + i + 1], (ny, nz)) for i in range(n)])
        near = [
            jnp.concatenate([v[1:], halo_x[r, 1, e][None]], axis=0),
            jnp.concatenate([halo_x[r, 0, e][None], v[:-1]], axis=0),
            jnp.where(y >= ny - s, hy, roll(v, -s, 1)),
            jnp.where(y < s, hy, roll(v, s, 1)),
            jnp.where(z >= nz - s, zh, roll(v, -s, 2)),
            jnp.where(z < s, zl, roll(v, s, 2)),
        ]
        total = weight(e, 0) * near[0]
        for k in range(1, 6):
            total = total + weight(e, k) * near[k]
        return total

    def coarsen(a, s):
        n = a.shape[0]
        a = jnp.stack([a[2 * i] + a[2 * i + 1] for i in range(n // 2)])
        y, z = iota(a.shape, 1), iota(a.shape, 2)
        a = a + jnp.where((y // s) % 2 == 0, roll(a, -s, 1), roll(a, s, 1))
        a = a + jnp.where((z // s) % 2 == 0, roll(a, -s, 2), roll(a, s, 2))
        return a * 0.125

    def spread(a):
        return jnp.stack([a[i // 2] for i in range(2 * a.shape[0])])

    def weight0(e, k):
        return w_ref[6 * e + k]

    def weight1(e, k):
        return w1[6 * e + k]

    source = iota((nz, nz), 0)
    target = iota((nz, nz), 1)
    squeeze = jnp.where(source == 4 * (target % qz), 1.0, 0.0).astype(jnp.float32)

    def to_rows(a):
        m = a.shape[0]
        c = jnp.dot(a.reshape(m * qx * ny, nz), squeeze, precision=HIGH,
                    preferred_element_type=jnp.float32).reshape(m, qx, ny, nz)
        shape = (m, ny, nz)
        lane = iota(shape, 2)
        got = jnp.zeros(shape, jnp.float32)
        for x in range(qx):
            for y in range(qy):
                part = roll(c[:, x], -4 * y, 1)
                got = jnp.where(lane // qz == x * qy + y, part, got)
        return got

    def own(small, whole, sem):
        return pltpu.make_async_copy(
            small.at[:, pl.ds(0, 1)], whole.at[X, core, :, pl.ds(row, 1)], sem
        )

    def stage(number, small, whole, ss, rs):
        made = []
        if number == 0:
            for step in range(1, ngy):
                made.append((small.at[:, pl.ds(0, 1)], whole.at[X, core, :, pl.ds(row, 1)],
                             step, device("gy", (gy + step) % ngy)))
        elif number == 1:
            block = whole.at[X, core, :, pl.ds(gx * ngy, ngy)]
            for step in range(1, ngx):
                made.append((block, block, step, device("gx", (gx + step) % ngx)))
        elif number == 2:
            block = whole.at[X, core]
            for step in range(1, nX):
                made.append((block, block, step, device("gz", ((X + step) % nX) * cores + core)))
        else:
            block = whole.at[:, core]
            for step in range(1, cores):
                made.append((block, block, step, device("gz", X * cores + (core + step) % cores)))
        return [
            pltpu.make_async_remote_copy(
                src_ref=a, dst_ref=z, send_sem=ss.at[number, step], recv_sem=rs.at[number, step],
                device_id=where, device_id_type=MESH,
            )
            for a, z, step, where in made
        ]

    wargs = (wsend, wall, ws_sem, wr_sem)
    bargs = (bsend, ball, bs_sem, br_sem)

    def start(number, args):
        for copy in stage(number, *args):
            copy.start()

    def finish(number, args):
        for copy in stage(number, *args):
            copy.wait_recv()

    v = [g_ref[e] for e in range(EQ)]
    send(0, v, nx, 1)
    for e in range(EQ):
        total = d_ref[e]
        for k in range(6):
            total = total + w_ref[6 * e + k]
        tot0[e] = total
        c0[e] = DAMP / total
        total = coarsen(d_ref[e], 1)
        wsend_d = coarsen(total, 2)
        for k in range(6):
            w = 0.25 * coarsen(w_ref[6 * e + k], 1)
            w1[6 * e + k] = w
            total = total + w
            wsend[6 * e + k] = to_rows((0.25 * coarsen(w, 2))[None])[0]
        wsend[6 * EQ + e] = to_rows(wsend_d[None])[0]
        tot1[e] = total
        c1[e] = DAMP / total
    own(wsend, wall, l_sem.at[0]).start()
    start(0, wargs)

    def smooth0(r, v):
        return [
            (1.0 - DAMP) * v[e] + c0[e] * (b_ref[e] + near_sum(r, v, e, nx, 1, weight0))
            for e in range(EQ)
        ]

    def smooth1(r, v):
        return [
            (1.0 - DAMP) * v[e] + c1[e] * (b1[e] + near_sum(r, v, e, nx // 2, 2, weight1))
            for e in range(EQ)
        ]

    receive(0, nx, 1)
    v = smooth0(0, v)
    send(1, v, nx, 1)
    receive(1, nx, 1)
    v = smooth0(1, v)
    send(2, v, nx, 1)
    own(wsend, wall, l_sem.at[0]).wait()
    finish(0, wargs)
    start(1, wargs)
    receive(2, nx, 1)
    u = []
    for e in range(EQ):
        rest = b_ref[e] - tot0[e] * v[e] + near_sum(2, v, e, nx, 1, weight0)
        b = coarsen(rest, 1)
        b1[e] = b
        u.append(c1[e] * b)
    half = nx // 2
    send(3, u, half, 2)
    finish(1, wargs)
    start(2, wargs)
    receive(3, half, 2)
    u = smooth1(3, u)
    send(4, u, half, 2)
    finish(2, wargs)
    start(3, wargs)
    receive(4, half, 2)
    for e in range(EQ):
        rest = b1[e] - tot1[e] * u[e] + near_sum(4, u, e, half, 2, weight1)
        bsend[e] = to_rows(coarsen(rest, 2)[None])[0]
    own(bsend, ball, l_sem.at[1]).start()
    start(0, bargs)
    finish(3, wargs)

    shape = (ngz, rows, nz)
    r_i, l_i = iota(shape, 1), iota(shape, 2)
    g_i = iota(shape, 0)
    zi, yi, xi = l_i % qz, (l_i // qz) % qy, l_i // (qz * qy)
    gyi, gxi = r_i % ngy, r_i // ngy
    inside = [
        ~((xi == qx - 1) & (gxi == ngx - 1)), ~((xi == 0) & (gxi == 0)),
        ~((yi == qy - 1) & (gyi == ngy - 1)), ~((yi == 0) & (gyi == 0)),
        ~((zi == qz - 1) & (g_i == ngz - 1)), ~((zi == 0) & (g_i == 0)),
    ]

    def whole(ref, index):
        return ref[:, :, index].reshape(shape)

    def next_of(v):
        return jnp.concatenate([v[1:], v[:1]], axis=0)

    def prev_of(v):
        return jnp.concatenate([v[-1:], v[:-1]], axis=0)

    def near2(v):
        sy, sx = qz, qz * qy
        return [
            jnp.where(xi == qx - 1, roll(roll(v, (qx - 1) * sx, 2), -ngy, 1), roll(v, -sx, 2)),
            jnp.where(xi == 0, roll(roll(v, -(qx - 1) * sx, 2), ngy, 1), roll(v, sx, 2)),
            jnp.where(yi == qy - 1, roll(roll(v, (qy - 1) * sy, 2), -1, 1), roll(v, -sy, 2)),
            jnp.where(yi == 0, roll(roll(v, -(qy - 1) * sy, 2), 1, 1), roll(v, sy, 2)),
            jnp.where(zi == qz - 1, roll(next_of(v), qz - 1, 2), roll(v, -1, 2)),
            jnp.where(zi == 0, roll(prev_of(v), -(qz - 1), 2), roll(v, 1, 2)),
        ]

    def dot_near(weights, near):
        total = weights[0] * near[0]
        for k in range(1, 6):
            total = total + weights[k] * near[k]
        return total

    def pair(a):
        sy, sx = qz, qz * qy
        a = a + jnp.where(xi % 2 == 0, roll(a, -sx, 2), roll(a, sx, 2))
        a = a + jnp.where(yi % 2 == 0, roll(a, -sy, 2), roll(a, sy, 2))
        a = a + jnp.where(zi % 2 == 0, roll(a, -1, 2), roll(a, 1, 2))
        return a * 0.125

    groups = qx * qy
    tiles = ngz // groups
    shape3 = (tiles, rows, nz)
    r3, l3, t3 = iota(shape3, 1), iota(shape3, 2), iota(shape3, 0)
    inside3 = [
        r3 // ngy < ngx - 1, r3 // ngy > 0, r3 % ngy < ngy - 1, r3 % ngy > 0,
        ~((l3 >= nz - 2) & (t3 == tiles - 1)), ~((l3 < 2) & (t3 == 0)),
    ]

    def join(a):
        a = a.reshape(tiles, groups, rows, nz)
        got = a[:, 0]
        for j in range(1, groups):
            got = jnp.where(l3 // qz == j, a[:, j], got)
        return got

    def part(a):
        parts = []
        for j in range(groups):
            mine = jnp.where(l3 // qz == j, a, 0.0)
            size = qz
            while size < nz:
                mine = mine + roll(mine, size, 2)
                size *= 2
            parts.append(mine)
        return jnp.stack(parts, axis=1).reshape(shape)

    def near3(v):
        if tiles == 1:
            up, down = roll(v, -2, 2), roll(v, 2, 2)
        else:
            up = jnp.where(l3 >= nz - 2, roll(next_of(v), -2, 2), roll(v, -2, 2))
            down = jnp.where(l3 < 2, roll(prev_of(v), 2, 2), roll(v, 2, 2))
        return [roll(v, -ngy, 1), roll(v, ngy, 1), roll(v, -1, 1), roll(v, 1, 1), up, down]

    w2, t2, w3, t3s = [], [], [], []
    for e in range(EQ):
        plain = [whole(wall, 6 * e + k) for k in range(6)]
        d2 = whole(wall, 6 * EQ + e)
        total = d2
        for k in range(6):
            total = total + plain[k]
        t2.append(total)
        w2.append([jnp.where(inside[k], plain[k], 0.0) for k in range(6)])
        plain3 = [0.25 * join(pair(plain[k])) for k in range(6)]
        total = join(pair(d2))
        for k in range(6):
            total = total + plain3[k]
        t3s.append(total)
        w3.append([jnp.where(inside3[k], plain3[k], 0.0) for k in range(6)])
    c2 = [DAMP / t for t in t2]
    c3 = [DAMP / t for t in t3s]

    own(bsend, ball, l_sem.at[1]).wait()
    finish(0, bargs)
    for number in range(1, 4):
        start(number, bargs)
        finish(number, bargs)

    keep = 1.0 - DAMP
    for e in range(EQ):
        rhs = whole(ball, e)
        v2 = c2[e] * rhs
        for step in range(SWEEPS - 1):
            v2 = keep * v2 + c2[e] * (rhs + dot_near(w2[e], near2(v2)))
        rest = rhs - t2[e] * v2 + dot_near(w2[e], near2(v2))
        rhs3 = join(pair(rest))
        v3 = c3[e] * rhs3
        for step in range(COARSE_SWEEPS - 1):
            v3 = keep * v3 + c3[e] * (rhs3 + dot_near(w3[e], near3(v3)))
        v2 = v2 + part(v3)
        for step in range(SWEEPS):
            v2 = keep * v2 + c2[e] * (rhs + dot_near(w2[e], near2(v2)))
        e2[e] = v2

    wide = groups * nz
    source = iota((nz, wide), 0)
    target = iota((nz, wide), 1)
    widen = jnp.where(source == (target // nz) * qz + (target % nz) // 4, 1.0, 0.0).astype(jnp.float32)
    back = jnp.concatenate(
        [jnp.broadcast_to(e2[e, gz, pl.ds(row, 1), :], (ny, nz)) for e in range(EQ)], axis=0
    )
    back = jnp.dot(back, widen, precision=HIGH, preferred_element_type=jnp.float32)
    ysel = iota((ny, nz), 0) // 4
    for e in range(EQ):
        planes = []
        for x in range(qx):
            got = back[e * ny : (e + 1) * ny, (x * qy) * nz : (x * qy + 1) * nz]
            for y in range(1, qy):
                col = (x * qy + y) * nz
                got = jnp.where(ysel == y, back[e * ny : (e + 1) * ny, col : col + nz], got)
            planes.append(got)
        u[e] = u[e] + spread(jnp.stack(planes))
    send(5, u, half, 2)
    receive(5, half, 2)
    u = smooth1(5, u)
    send(6, u, half, 2)
    receive(6, half, 2)
    u = smooth1(6, u)
    v = [field[2, e] + spread(u[e]) for e in range(EQ)]
    send(7, v, nx, 1)
    receive(7, nx, 1)
    v = smooth0(7, v)
    send(8, v, nx, 1)
    receive(8, nx, 1)
    v = smooth0(8, v)
    for e in range(EQ):
        out_ref[e] = v[e]

    for r in range(rounds):
        n, s = (half, 2) if 3 <= r <= 6 else (nx, 1)
        for copy, has_target, _ in copies(r, n, s):
            @pl.when(has_target)
            def _():
                copy.wait_send()
    for args in (wargs, bargs):
        for number in range(4):
            for copy in stage(number, *args):
                copy.wait_send()


def per_device(dims, cores, couplings, diagonal, right_side, guess):
    ngx, ngy, ngz = dims
    brick = guess.shape[1:]
    nx, ny, nz = brick
    half = nx // 2
    rows = ngx * ngy
    nX = ngz // cores
    rounds = 9
    peers = max(ngx, ngy, nX, cores)
    f32 = jnp.float32
    vmem = pltpu.VMEM
    dma = pltpu.SemaphoreType.DMA
    return pl.pallas_call(
        functools.partial(kernel, dims, cores),
        out_shape=jax.ShapeDtypeStruct(guess.shape, f32),
        in_specs=[pl.BlockSpec(memory_space=vmem)] * 4,
        out_specs=pl.BlockSpec(memory_space=vmem),
        scratch_shapes=[
            vmem((rounds, EQ) + brick, f32),
            vmem((rounds, 2, EQ, ny, nz), f32),
            vmem((rounds, EQ) + brick, f32),
            vmem((rounds, 2, ny, nz), f32),
            vmem((rounds, 2, ny, nz), f32),
            vmem((EQ,) + brick, f32),
            vmem((EQ,) + brick, f32),
            vmem((6 * EQ, half, ny, nz), f32),
            vmem((EQ, half, ny, nz), f32),
            vmem((EQ, half, ny, nz), f32),
            vmem((EQ, half, ny, nz), f32),
            vmem((7 * EQ, ny, nz), f32),
            vmem((nX, cores, 7 * EQ, rows, nz), f32),
            vmem((EQ, ny, nz), f32),
            vmem((nX, cores, EQ, rows, nz), f32),
            vmem((EQ, ngz, rows, nz), f32),
            dma((rounds, 6)),
            dma((rounds, 6)),
            dma((4, peers)),
            dma((4, peers)),
            dma((4, peers)),
            dma((4, peers)),
            dma((2,)),
        ],
        compiler_params=pltpu.CompilerParams(
            collective_id=0, has_side_effects=True, vmem_limit_bytes=60 * 1024 * 1024
        ),
    )(couplings, diagonal, right_side, guess)


def solution(mesh):
    dims = (mesh.shape["gx"], mesh.shape["gy"], mesh.shape["gz"])
    cores = 2 if dims[2] % 2 == 0 else 1
    spec = P(None, "gx", "gy", "gz")
    return jax.shard_map(
        functools.partial(per_device, dims, cores),
        mesh=mesh,
        in_specs=(spec,) * 4,
        out_specs=spec,
        check_vma=False,
    )
```

```python
import functools

import jax
import jax.numpy as jnp
from jax import lax
from jax.experimental import pallas as pl
from jax.experimental.pallas import tpu as pltpu
from jax.sharding import PartitionSpec as P

SWEEPS = 2
COARSE_SWEEPS = 8
DAMP = 0.8
EQ = 3
MESH = pl.DeviceIdType.MESH
HIGH = lax.Precision.HIGHEST


def roll(value, shift, axis):
    size = value.shape[axis]
    shift = shift % size
    return value if shift == 0 else pltpu.roll(value, shift, axis)


def iota(shape, axis):
    return lax.broadcasted_iota(jnp.int32, shape, axis)


def kernel(
    dims, cores, w_ref, d_ref, b_ref, g_ref, out_ref,
    field, halo_x, halo_y, pack_s, pack_r, tot0, c0, w1, tot1, c1, b1,
    wsend, wall, bsend, ball, e2, lines,
    s_sem, r_sem, ws_sem, wr_sem, bs_sem, br_sem, l_sem,
):
    ngx, ngy, ngz = dims
    nx, ny, nz = g_ref.shape[1:]
    qx, qy, qz = nx // 4, ny // 4, nz // 4
    rows = ngx * ngy
    nX = ngz // cores
    gx, gy, gz = lax.axis_index("gx"), lax.axis_index("gy"), lax.axis_index("gz")
    X, core = gz // cores, gz % cores
    row = gy * ngx + gx
    axes = (("gx", gx, ngx), ("gy", gy, ngy), ("gz", gz, ngz))

    def device(name, index):
        here = {"gx": gx, "gy": gy, "gz": gz}
        here[name] = index
        return (here["gx"], here["gy"], here["gz"])

    barrier = pltpu.get_barrier_semaphore()
    close = ngy <= 4 and ngz <= 4
    awaited = 0
    for name, index, count in axes:
        if close and name != "gx":
            for step in (-1, 1):
                @pl.when((index + step >= 0) & (index + step < count))
                def _():
                    pl.semaphore_signal(
                        barrier, inc=1, device_id=device(name, jnp.clip(index + step, 0, count - 1)),
                        device_id_type=MESH,
                    )
            awaited = awaited + (index > 0).astype(jnp.int32) + (index < count - 1).astype(jnp.int32)
        else:
            for step in range(1, count):
                pl.semaphore_signal(
                    barrier, inc=1, device_id=device(name, (index + step) % count), device_id_type=MESH
                )
            awaited = awaited + (count - 1)

    rounds = field.shape[0]
    for name, index, count in axes:
        for side in range(2):
            @pl.when(index == (0 if side == 0 else count - 1))
            def _():
                for r in range(rounds):
                    if name == "gx":
                        halo_x[r, side] = jnp.zeros(halo_x.shape[2:], jnp.float32)
                    elif name == "gy":
                        lo = 0 if side == 0 else ny // 2
                        halo_y[r, :, :, lo : lo + ny // 2] = jnp.zeros(
                            (EQ, nx, ny // 2, nz), jnp.float32
                        )
                    else:
                        pack_r[r, side] = jnp.zeros(pack_r.shape[2:], jnp.float32)

    pl.semaphore_wait(barrier, awaited)

    lane2 = iota((ny, nz), 1)

    def copies(r, n, s):
        src = g_ref if r == 0 else field.at[r]
        made = []
        for side in range(2):
            other = 1 - side
            for place, (name, index, count) in enumerate(axes):
                if name == "gx":
                    a = src.at[:, 0 if side == 0 else n - 1]
                    z = halo_x.at[r, other]
                elif name == "gy":
                    a = src.at[:, 0:n, pl.ds(0 if side == 0 else ny - s, s)]
                    z = halo_y.at[r, :, 0:n, pl.ds(ny - s if side == 0 else 0, s)]
                else:
                    a = pack_s.at[r, side]
                    z = pack_r.at[r, other]
                target = index - 1 if side == 0 else index + 1
                has_target = index > 0 if side == 0 else index < count - 1
                has_source = index < count - 1 if side == 0 else index > 0
                slot = 2 * place + side
                made.append((
                    pltpu.make_async_remote_copy(
                        src_ref=a, dst_ref=z,
                        send_sem=s_sem.at[r, slot], recv_sem=r_sem.at[r, slot],
                        device_id=device(name, jnp.clip(target, 0, count - 1)),
                        device_id_type=MESH,
                    ),
                    has_target, has_source,
                ))
        return made

    def send(r, value, n, s):
        low = jnp.zeros((ny, nz), jnp.float32)
        high = jnp.zeros((ny, nz), jnp.float32)
        for e in range(EQ):
            if r > 0:
                field[r, e, 0:n] = value[e]
            for i in range(n):
                here = lane2 == e * n + i
                low = jnp.where(here, jnp.broadcast_to(value[e][i, :, 0:1], (ny, nz)), low)
                high = jnp.where(here, jnp.broadcast_to(value[e][i, :, nz - 1 : nz], (ny, nz)), high)
        pack_s[r, 0] = low
        pack_s[r, 1] = high
        for copy, has_target, _ in copies(r, n, s):
            @pl.when(has_target)
            def _():
                copy.start()

    def receive(r, n, s):
        for copy, _, has_source in copies(r, n, s):
            @pl.when(has_source)
            def _():
                copy.wait_recv()

    def near_sum(r, value, e, n, s, weight):
        v = value[e]
        shape = (n, ny, nz)
        y, z = iota(shape, 1), iota(shape, 2)
        hy = halo_y[r, e, 0:n]
        low = pack_r[r, 0]
        high = pack_r[r, 1]
        zl = jnp.stack([jnp.broadcast_to(low[:, e * n + i : e * n + i + 1], (ny, nz)) for i in range(n)])
        zh = jnp.stack([jnp.broadcast_to(high[:, e * n + i : e * n + i + 1], (ny, nz)) for i in range(n)])
        near = [
            jnp.concatenate([v[1:], halo_x[r, 1, e][None]], axis=0),
            jnp.concatenate([halo_x[r, 0, e][None], v[:-1]], axis=0),
            jnp.where(y >= ny - s, hy, roll(v, -s, 1)),
            jnp.where(y < s, hy, roll(v, s, 1)),
            jnp.where(z >= nz - s, zh, roll(v, -s, 2)),
            jnp.where(z < s, zl, roll(v, s, 2)),
        ]
        total = weight(e, 0) * near[0]
        for k in range(1, 6):
            total = total + weight(e, k) * near[k]
        return total

    def coarsen(a, s):
        n = a.shape[0]
        a = jnp.stack([a[2 * i] + a[2 * i + 1] for i in range(n // 2)])
        y, z = iota(a.shape, 1), iota(a.shape, 2)
        a = a + jnp.where((y // s) % 2 == 0, roll(a, -s, 1), roll(a, s, 1))
        a = a + jnp.where((z // s) % 2 == 0, roll(a, -s, 2), roll(a, s, 2))
        return a * 0.125

    def spread(a):
        return jnp.stack([a[i // 2] for i in range(2 * a.shape[0])])

    def weight0(e, k):
        return w_ref[6 * e + k]

    def weight1(e, k):
        return w1[6 * e + k]

    source = iota((nz, nz), 0)
    target = iota((nz, nz), 1)
    squeeze = jnp.where(source == 4 * (target % qz), 1.0, 0.0).astype(jnp.float32)

    def to_rows(a):
        m = a.shape[0]
        c = jnp.dot(a.reshape(m * qx * ny, nz), squeeze, precision=HIGH,
                    preferred_element_type=jnp.float32).reshape(m, qx, ny, nz)
        shape = (m, ny, nz)
        lane = iota(shape, 2)
        got = jnp.zeros(shape, jnp.float32)
        for x in range(qx):
            for y in range(qy):
                part = roll(c[:, x], -4 * y, 1)
                got = jnp.where(lane // qz == x * qy + y, part, got)
        return got

    def own(small, whole, sem):
        return pltpu.make_async_copy(
            small.at[:, pl.ds(0, 1)], whole.at[X, core, :, pl.ds(row, 1)], sem
        )

    def stage(number, small, whole, ss, rs):
        made = []
        if number == 0:
            for step in range(1, ngx):
                made.append((small.at[:, pl.ds(0, 1)], whole.at[X, core, :, pl.ds(row, 1)],
                             step, device("gx", (gx + step) % ngx)))
        elif number == 1:
            block = whole.at[X, core, :, pl.ds(gy * ngx, ngx)]
            for step in range(1, ngy):
                made.append((block, block, step, device("gy", (gy + step) % ngy)))
        elif number == 2:
            block = whole.at[X, core]
            for step in range(1, nX):
                made.append((block, block, step, device("gz", ((X + step) % nX) * cores + core)))
        else:
            block = whole.at[:, core]
            for step in range(1, cores):
                made.append((block, block, step, device("gz", X * cores + (core + step) % cores)))
        return [
            pltpu.make_async_remote_copy(
                src_ref=a, dst_ref=z, send_sem=ss.at[number, step], recv_sem=rs.at[number, step],
                device_id=where, device_id_type=MESH,
            )
            for a, z, step, where in made
        ]

    wargs = (wsend, wall, ws_sem, wr_sem)

    def everyone():
        made = []
        for az in range(ngz):
            for ay in range(ngy):
                for ax in range(ngx):
                    if ax + ay + az == 0:
                        continue
                    made.append(pltpu.make_async_remote_copy(
                        src_ref=bsend.at[:, pl.ds(0, 1)],
                        dst_ref=ball.at[X, core, :, pl.ds(row, 1)],
                        send_sem=bs_sem, recv_sem=br_sem,
                        device_id=((gx + ax) % ngx, (gy + ay) % ngy, (gz + az) % ngz),
                        device_id_type=MESH,
                    ))
        return made

    def start(number, args):
        for copy in stage(number, *args):
            copy.start()

    def finish(number, args):
        for copy in stage(number, *args):
            copy.wait_recv()

    v = [g_ref[e] for e in range(EQ)]
    send(0, v, nx, 1)
    for e in range(EQ):
        total = d_ref[e]
        for k in range(6):
            total = total + w_ref[6 * e + k]
        tot0[e] = total
        c0[e] = DAMP / total
        total = coarsen(d_ref[e], 1)
        wsend_d = coarsen(total, 2)
        for k in range(6):
            w = 0.25 * coarsen(w_ref[6 * e + k], 1)
            w1[6 * e + k] = w
            total = total + w
            wsend[6 * e + k] = to_rows((0.25 * coarsen(w, 2))[None])[0]
        wsend[6 * EQ + e] = to_rows(wsend_d[None])[0]
        tot1[e] = total
        c1[e] = DAMP / total
    own(wsend, wall, l_sem.at[0]).start()
    start(0, wargs)

    def smooth0(r, v):
        return [
            (1.0 - DAMP) * v[e] + c0[e] * (b_ref[e] + near_sum(r, v, e, nx, 1, weight0))
            for e in range(EQ)
        ]

    def smooth1(r, v):
        return [
            (1.0 - DAMP) * v[e] + c1[e] * (b1[e] + near_sum(r, v, e, nx // 2, 2, weight1))
            for e in range(EQ)
        ]

    receive(0, nx, 1)
    v = smooth0(0, v)
    send(1, v, nx, 1)
    receive(1, nx, 1)
    own(wsend, wall, l_sem.at[0]).wait()
    finish(0, wargs)
    start(1, wargs)
    v = smooth0(1, v)
    send(2, v, nx, 1)
    receive(2, nx, 1)
    u = []
    for e in range(EQ):
        rest = b_ref[e] - tot0[e] * v[e] + near_sum(2, v, e, nx, 1, weight0)
        b = coarsen(rest, 1)
        b1[e] = b
        u.append(c1[e] * b)
    half = nx // 2
    send(3, u, half, 2)
    receive(3, half, 2)
    u = smooth1(3, u)
    finish(1, wargs)
    send(4, u, half, 2)
    start(2, wargs)
    receive(4, half, 2)
    for e in range(EQ):
        rest = b1[e] - tot1[e] * u[e] + near_sum(4, u, e, half, 2, weight1)
        bsend[e] = to_rows(coarsen(rest, 2)[None])[0]
    for copy in everyone():
        copy.start()
    own(bsend, ball, br_sem).start()
    finish(2, wargs)
    start(3, wargs)
    finish(3, wargs)

    shape = (ngz, rows, nz)
    r_i, l_i = iota(shape, 1), iota(shape, 2)
    g_i = iota(shape, 0)
    zi, yi, xi = l_i % qz, (l_i // qz) % qy, l_i // (qz * qy)
    gyi, gxi = r_i // ngx, r_i % ngx
    inside = [
        ~((xi == qx - 1) & (gxi == ngx - 1)), ~((xi == 0) & (gxi == 0)),
        ~((yi == qy - 1) & (gyi == ngy - 1)), ~((yi == 0) & (gyi == 0)),
        ~((zi == qz - 1) & (g_i == ngz - 1)), ~((zi == 0) & (g_i == 0)),
    ]

    def whole(ref, index):
        return ref[:, :, index].reshape(shape)

    def next_of(v):
        return jnp.concatenate([v[1:], v[:1]], axis=0)

    def prev_of(v):
        return jnp.concatenate([v[-1:], v[:-1]], axis=0)

    def near2(v):
        sy, sx = qz, qz * qy
        return [
            jnp.where(xi == qx - 1, roll(roll(v, (qx - 1) * sx, 2), -1, 1), roll(v, -sx, 2)),
            jnp.where(xi == 0, roll(roll(v, -(qx - 1) * sx, 2), 1, 1), roll(v, sx, 2)),
            jnp.where(yi == qy - 1, roll(roll(v, (qy - 1) * sy, 2), -ngx, 1), roll(v, -sy, 2)),
            jnp.where(yi == 0, roll(roll(v, -(qy - 1) * sy, 2), ngx, 1), roll(v, sy, 2)),
            jnp.where(zi == qz - 1, roll(next_of(v), qz - 1, 2), roll(v, -1, 2)),
            jnp.where(zi == 0, roll(prev_of(v), -(qz - 1), 2), roll(v, 1, 2)),
        ]

    def dot_near(weights, near):
        total = weights[0] * near[0]
        for k in range(1, 6):
            total = total + weights[k] * near[k]
        return total

    def pair(a):
        sy, sx = qz, qz * qy
        a = a + jnp.where(xi % 2 == 0, roll(a, -sx, 2), roll(a, sx, 2))
        a = a + jnp.where(yi % 2 == 0, roll(a, -sy, 2), roll(a, sy, 2))
        a = a + jnp.where(zi % 2 == 0, roll(a, -1, 2), roll(a, 1, 2))
        return a * 0.125

    groups = qx * qy
    tiles = ngz // groups
    shape3 = (tiles, rows, nz)
    r3, l3, t3 = iota(shape3, 1), iota(shape3, 2), iota(shape3, 0)
    inside3 = [
        r3 % ngx < ngx - 1, r3 % ngx > 0, r3 // ngx < ngy - 1, r3 // ngx > 0,
        ~((l3 >= nz - 2) & (t3 == tiles - 1)), ~((l3 < 2) & (t3 == 0)),
    ]

    def join(a):
        a = a.reshape(tiles, groups, rows, nz)
        got = a[:, 0]
        for j in range(1, groups):
            got = jnp.where(l3 // qz == j, a[:, j], got)
        return got

    def part(a):
        parts = []
        for j in range(groups):
            mine = jnp.where(l3 // qz == j, a, 0.0)
            size = qz
            while size < nz:
                mine = mine + roll(mine, size, 2)
                size *= 2
            parts.append(mine)
        return jnp.stack(parts, axis=1).reshape(shape)

    def near3(v):
        if tiles == 1:
            up, down = roll(v, -2, 2), roll(v, 2, 2)
        else:
            up = jnp.where(l3 >= nz - 2, roll(next_of(v), -2, 2), roll(v, -2, 2))
            down = jnp.where(l3 < 2, roll(prev_of(v), 2, 2), roll(v, 2, 2))
        return [roll(v, -1, 1), roll(v, 1, 1), roll(v, -ngx, 1), roll(v, ngx, 1), up, down]

    w2, t2, w3, t3s = [], [], [], []
    for e in range(EQ):
        plain = [whole(wall, 6 * e + k) for k in range(6)]
        d2 = whole(wall, 6 * EQ + e)
        total = d2
        for k in range(6):
            total = total + plain[k]
        t2.append(total)
        w2.append([jnp.where(inside[k], plain[k], 0.0) for k in range(6)])
        plain3 = [0.25 * join(pair(plain[k])) for k in range(6)]
        total = join(pair(d2))
        for k in range(6):
            total = total + plain3[k]
        t3s.append(total)
        w3.append([jnp.where(inside3[k], plain3[k], 0.0) for k in range(6)])
    c2 = [DAMP / t for t in t2]
    c3 = [DAMP / t for t in t3s]

    pltpu.make_async_copy(ball, ball, br_sem).wait()

    keep = 1.0 - DAMP
    for e in range(EQ):
        rhs = whole(ball, e)
        v2 = c2[e] * rhs
        for step in range(SWEEPS - 1):
            v2 = keep * v2 + c2[e] * (rhs + dot_near(w2[e], near2(v2)))
        rest = rhs - t2[e] * v2 + dot_near(w2[e], near2(v2))
        rhs3 = join(pair(rest))
        v3 = c3[e] * rhs3
        for step in range(COARSE_SWEEPS - 1):
            v3 = keep * v3 + c3[e] * (rhs3 + dot_near(w3[e], near3(v3)))
        v2 = v2 + part(v3)
        for step in range(SWEEPS):
            v2 = keep * v2 + c2[e] * (rhs + dot_near(w2[e], near2(v2)))
        e2[e] = v2

    wide = groups * nz
    source = iota((nz, wide), 0)
    target = iota((nz, wide), 1)
    widen = jnp.where(source == (target // nz) * qz + (target % nz) // 4, 1.0, 0.0).astype(jnp.float32)
    around = [(gx, gy, gz, None)]
    for axis, index, count in ((0, gx, ngx), (1, gy, ngy), (2, gz, ngz)):
        for step in (-1, 1):
            at = [gx, gy, gz]
            at[axis] = jnp.clip(index + step, 0, count - 1)
            has = index > 0 if step < 0 else index < count - 1
            around.append((at[0], at[1], at[2], has))
    for e in range(EQ):
        for j, (ax, ay, az, has) in enumerate(around):
            line = e2[e, az, pl.ds(ay * ngx + ax, 1), :]
            if has is not None:
                line = jnp.where(has, line, 0.0)
            lines[e * 7 + j : e * 7 + j + 1, :] = line
    for j in range(EQ * 7, lines.shape[0]):
        lines[j : j + 1, :] = jnp.zeros((1, nz), jnp.float32)
    back = jnp.dot(lines[...], widen, precision=HIGH, preferred_element_type=jnp.float32)
    ysel = iota((ny, nz), 0) // 4

    def strip(e, j, x, y):
        col = (x * qy + y) * nz
        return jnp.broadcast_to(back[e * 7 + j : e * 7 + j + 1, col : col + nz], (ny, nz))

    def plane(e, j, x):
        got = strip(e, j, x, 0)
        for y in range(1, qy):
            got = jnp.where(ysel == y, strip(e, j, x, y), got)
        return got

    low, high = pack_r[4, 0], pack_r[4, 1]
    for e in range(EQ):
        halo_x[5, 0, e] = halo_x[4, 0, e] + plane(e, 1, qx - 1)
        halo_x[5, 1, e] = halo_x[4, 1, e] + plane(e, 2, 0)
        for x in range(qx):
            edge = jnp.where(ysel < qy // 2, strip(e, 3, x, qy - 1), strip(e, 4, x, 0))
            below, above = plane(e, 5, x), plane(e, 6, x)
            for i in (2 * x, 2 * x + 1):
                halo_y[5, e, i] = halo_y[4, e, i] + edge
                here = lane2 == e * half + i
                low = jnp.where(here, low + jnp.broadcast_to(below[:, nz - 1 : nz], (ny, nz)), low)
                high = jnp.where(here, high + jnp.broadcast_to(above[:, 0:1], (ny, nz)), high)
        u[e] = u[e] + spread(jnp.stack([plane(e, 0, x) for x in range(qx)]))
    pack_r[5, 0] = low
    pack_r[5, 1] = high
    u = smooth1(5, u)
    send(6, u, half, 2)
    receive(6, half, 2)
    u = smooth1(6, u)
    v = [field[2, e] + spread(u[e]) for e in range(EQ)]
    send(7, v, nx, 1)
    receive(7, nx, 1)
    v = smooth0(7, v)
    send(8, v, nx, 1)
    receive(8, nx, 1)
    v = smooth0(8, v)
    for e in range(EQ):
        out_ref[e] = v[e]

    for r in range(rounds):
        if r == 5:
            continue
        n, s = (half, 2) if 3 <= r <= 6 else (nx, 1)
        for copy, has_target, _ in copies(r, n, s):
            @pl.when(has_target)
            def _():
                copy.wait_send()
    for number in range(4):
        for copy in stage(number, *wargs):
            copy.wait_send()
    for copy in everyone():
        copy.wait_send()


def per_device(dims, cores, couplings, diagonal, right_side, guess):
    ngx, ngy, ngz = dims
    brick = guess.shape[1:]
    nx, ny, nz = brick
    half = nx // 2
    rows = ngx * ngy
    nX = ngz // cores
    rounds = 9
    peers = max(ngx, ngy, nX, cores)
    f32 = jnp.float32
    vmem = pltpu.VMEM
    dma = pltpu.SemaphoreType.DMA
    return pl.pallas_call(
        functools.partial(kernel, dims, cores),
        out_shape=jax.ShapeDtypeStruct(guess.shape, f32),
        in_specs=[pl.BlockSpec(memory_space=vmem)] * 4,
        out_specs=pl.BlockSpec(memory_space=vmem),
        scratch_shapes=[
            vmem((rounds, EQ) + brick, f32),
            vmem((rounds, 2, EQ, ny, nz), f32),
            vmem((rounds, EQ) + brick, f32),
            vmem((rounds, 2, ny, nz), f32),
            vmem((rounds, 2, ny, nz), f32),
            vmem((EQ,) + brick, f32),
            vmem((EQ,) + brick, f32),
            vmem((6 * EQ, half, ny, nz), f32),
            vmem((EQ, half, ny, nz), f32),
            vmem((EQ, half, ny, nz), f32),
            vmem((EQ, half, ny, nz), f32),
            vmem((7 * EQ, ny, nz), f32),
            vmem((nX, cores, 7 * EQ, rows, nz), f32),
            vmem((EQ, ny, nz), f32),
            vmem((nX, cores, EQ, rows, nz), f32),
            vmem((EQ, ngz, rows, nz), f32),
            vmem((-(-EQ * 7 // 8) * 8, nz), f32),
            dma((rounds, 6)),
            dma((rounds, 6)),
            dma((4, peers)),
            dma((4, peers)),
            dma,
            dma,
            dma((1,)),
        ],
        compiler_params=pltpu.CompilerParams(
            collective_id=0, has_side_effects=True, vmem_limit_bytes=60 * 1024 * 1024
        ),
    )(couplings, diagonal, right_side, guess)


def solution(mesh):
    dims = (mesh.shape["gx"], mesh.shape["gy"], mesh.shape["gz"])
    cores = 2 if dims[2] % 2 == 0 else 1
    spec = P(None, "gx", "gy", "gz")
    return jax.shard_map(
        functools.partial(per_device, dims, cores),
        mesh=mesh,
        in_specs=(spec,) * 4,
        out_specs=spec,
        check_vma=False,
    )
```

```python
import functools

import jax
import jax.numpy as jnp
from jax import lax
from jax.experimental import pallas as pl
from jax.experimental.pallas import tpu as pltpu
from jax.sharding import PartitionSpec as P

SWEEPS = 2
COARSE_SWEEPS = 8
DAMP = 0.8
EQ = 3
MESH = pl.DeviceIdType.MESH
HIGH = lax.Precision.HIGHEST


def roll(value, shift, axis):
    size = value.shape[axis]
    shift = shift % size
    return value if shift == 0 else pltpu.roll(value, shift, axis)


def iota(shape, axis):
    return lax.broadcasted_iota(jnp.int32, shape, axis)


def kernel(
    dims, cores, w_ref, d_ref, b_ref, g_ref, out_ref,
    field, halo_x, halo_y, pack_s, pack_r, tot0, c0, w1, tot1, c1, b1,
    wsend, wall, bsend, ball, e2, lines,
    s_sem, r_sem, ws_sem, wr_sem, bs_sem, br_sem, l_sem,
):
    ngx, ngy, ngz = dims
    nx, ny, nz = g_ref.shape[1:]
    qx, qy, qz = nx // 4, ny // 4, nz // 4
    rows = ngx * ngy
    nX = ngz // cores
    gx, gy, gz = lax.axis_index("gx"), lax.axis_index("gy"), lax.axis_index("gz")
    X, core = gz // cores, gz % cores
    row = gy * ngx + gx
    axes = (("gx", gx, ngx), ("gy", gy, ngy), ("gz", gz, ngz))

    def device(name, index):
        here = {"gx": gx, "gy": gy, "gz": gz}
        here[name] = index
        return (here["gx"], here["gy"], here["gz"])

    barrier = pltpu.get_barrier_semaphore()
    close = ngy <= 4 and ngz <= 4
    awaited = 0
    for name, index, count in axes:
        if close and name != "gx":
            for step in (-1, 1):
                @pl.when((index + step >= 0) & (index + step < count))
                def _():
                    pl.semaphore_signal(
                        barrier, inc=1, device_id=device(name, jnp.clip(index + step, 0, count - 1)),
                        device_id_type=MESH,
                    )
            awaited = awaited + (index > 0).astype(jnp.int32) + (index < count - 1).astype(jnp.int32)
        else:
            for step in range(1, count):
                pl.semaphore_signal(
                    barrier, inc=1, device_id=device(name, (index + step) % count), device_id_type=MESH
                )
            awaited = awaited + (count - 1)

    rounds = field.shape[0]
    for name, index, count in axes:
        for side in range(2):
            @pl.when(index == (0 if side == 0 else count - 1))
            def _():
                for r in range(rounds):
                    if name == "gx":
                        halo_x[r, side] = jnp.zeros(halo_x.shape[2:], jnp.float32)
                    elif name == "gy":
                        lo = 0 if side == 0 else ny // 2
                        halo_y[r, :, :, lo : lo + ny // 2] = jnp.zeros(
                            (EQ, nx, ny // 2, nz), jnp.float32
                        )
                    else:
                        pack_r[r, side] = jnp.zeros(pack_r.shape[2:], jnp.float32)

    pl.semaphore_wait(barrier, awaited)

    lane2 = iota((ny, nz), 1)

    def copies(r, n, s):
        src = g_ref if r == 0 else field.at[r]
        made = []
        for side in range(2):
            other = 1 - side
            for place, (name, index, count) in enumerate(axes):
                if name == "gx":
                    a = src.at[:, 0 if side == 0 else n - 1]
                    z = halo_x.at[r, other]
                elif name == "gy":
                    a = src.at[:, 0:n, pl.ds(0 if side == 0 else ny - s, s)]
                    z = halo_y.at[r, :, 0:n, pl.ds(ny - s if side == 0 else 0, s)]
                else:
                    a = pack_s.at[r, side]
                    z = pack_r.at[r, other]
                target = index - 1 if side == 0 else index + 1
                has_target = index > 0 if side == 0 else index < count - 1
                has_source = index < count - 1 if side == 0 else index > 0
                slot = 2 * place + side
                made.append((
                    pltpu.make_async_remote_copy(
                        src_ref=a, dst_ref=z,
                        send_sem=s_sem.at[r, slot], recv_sem=r_sem.at[r, slot],
                        device_id=device(name, jnp.clip(target, 0, count - 1)),
                        device_id_type=MESH,
                    ),
                    has_target, has_source, name,
                ))
        return made

    def send(r, value, n, s):
        made = copies(r, n, s)
        if r > 0:
            for e in range(EQ):
                field[r, e, 0:n] = value[e]
        for copy, has_target, _, name in made:
            if name != "gz":
                @pl.when(has_target)
                def _():
                    copy.start()
        low = jnp.zeros((ny, nz), jnp.float32)
        high = jnp.zeros((ny, nz), jnp.float32)
        for e in range(EQ):
            for i in range(n):
                here = lane2 == e * n + i
                low = jnp.where(here, jnp.broadcast_to(value[e][i, :, 0:1], (ny, nz)), low)
                high = jnp.where(here, jnp.broadcast_to(value[e][i, :, nz - 1 : nz], (ny, nz)), high)
        pack_s[r, 0] = low
        pack_s[r, 1] = high
        for copy, has_target, _, name in made:
            if name == "gz":
                @pl.when(has_target)
                def _():
                    copy.start()

    def receive(r, n, s):
        for copy, _, has_source, _ in copies(r, n, s):
            @pl.when(has_source)
            def _():
                copy.wait_recv()

    def before(v, e, n, s, weight, base, scale):
        shape = (n, ny, nz)
        y, z = iota(shape, 1), iota(shape, 2)
        edge = jnp.zeros((1, ny, nz), jnp.float32)
        near = [
            jnp.concatenate([v[1:], edge], axis=0),
            jnp.concatenate([edge, v[:-1]], axis=0),
            jnp.where(y >= ny - s, 0.0, roll(v, -s, 1)),
            jnp.where(y < s, 0.0, roll(v, s, 1)),
            jnp.where(z >= nz - s, 0.0, roll(v, -s, 2)),
            jnp.where(z < s, 0.0, roll(v, s, 2)),
        ]
        w = [weight(e, k) for k in range(6)]
        total = w[0] * near[0]
        for k in range(1, 6):
            total = total + w[k] * near[k]
        wy = jnp.where(y >= ny - s, w[2], jnp.where(y < s, w[3], 0.0))
        wz = jnp.where(z >= nz - s, w[4], jnp.where(z < s, w[5], 0.0))
        up, down = w[0][n - 1], w[1][0]
        if scale is not None:
            total, wy, wz = scale * total, scale * wy, scale * wz
            up, down = scale[n - 1] * up, scale[0] * down
        return base + total, up, down, wy, wz

    def after(r, e, n, s, ready):
        total, up, down, wy, wz = ready
        shape = (n, ny, nz)
        y, z = iota(shape, 1), iota(shape, 2)
        low = pack_r[r, 0]
        high = pack_r[r, 1]
        zl = jnp.stack([jnp.broadcast_to(low[:, e * n + i : e * n + i + 1], (ny, nz)) for i in range(n)])
        zh = jnp.stack([jnp.broadcast_to(high[:, e * n + i : e * n + i + 1], (ny, nz)) for i in range(n)])
        hy = jnp.where((y < s) | (y >= ny - s), halo_y[r, e, 0:n], 0.0)
        total = total + wy * hy + wz * jnp.where(z < s, zl, zh)
        first = total[0] + down * halo_x[r, 0, e]
        last = total[n - 1] + up * halo_x[r, 1, e]
        return jnp.concatenate([first[None], total[1 : n - 1], last[None]], axis=0)

    def coarsen(a, s):
        n = a.shape[0]
        a = jnp.stack([a[2 * i] + a[2 * i + 1] for i in range(n // 2)])
        y, z = iota(a.shape, 1), iota(a.shape, 2)
        a = a + jnp.where((y // s) % 2 == 0, roll(a, -s, 1), roll(a, s, 1))
        a = a + jnp.where((z // s) % 2 == 0, roll(a, -s, 2), roll(a, s, 2))
        return a * 0.125

    def spread(a):
        return jnp.stack([a[i // 2] for i in range(2 * a.shape[0])])

    def weight0(e, k):
        return w_ref[6 * e + k]

    def weight1(e, k):
        return w1[6 * e + k]

    source = iota((nz, nz), 0)
    target = iota((nz, nz), 1)
    squeeze = jnp.where(source == 4 * (target % qz), 1.0, 0.0).astype(jnp.float32)

    def to_rows(a):
        m = a.shape[0]
        c = jnp.dot(a.reshape(m * qx * ny, nz), squeeze, precision=HIGH,
                    preferred_element_type=jnp.float32).reshape(m, qx, ny, nz)
        shape = (m, ny, nz)
        lane = iota(shape, 2)
        got = jnp.zeros(shape, jnp.float32)
        for x in range(qx):
            for y in range(qy):
                part = roll(c[:, x], -4 * y, 1)
                got = jnp.where(lane // qz == x * qy + y, part, got)
        return got

    def own(small, whole, sem):
        return pltpu.make_async_copy(
            small.at[:, pl.ds(0, 1)], whole.at[X, core, :, pl.ds(row, 1)], sem
        )

    def stage(number, small, whole, ss, rs):
        made = []
        if number == 0:
            for step in range(1, ngx):
                made.append((small.at[:, pl.ds(0, 1)], whole.at[X, core, :, pl.ds(row, 1)],
                             step, device("gx", (gx + step) % ngx)))
        elif number == 1:
            block = whole.at[X, core, :, pl.ds(gy * ngx, ngx)]
            for step in range(1, ngy):
                made.append((block, block, step, device("gy", (gy + step) % ngy)))
        elif number == 2:
            block = whole.at[X, core]
            for step in range(1, nX):
                made.append((block, block, step, device("gz", ((X + step) % nX) * cores + core)))
        else:
            block = whole.at[:, core]
            for step in range(1, cores):
                made.append((block, block, step, device("gz", X * cores + (core + step) % cores)))
        return [
            pltpu.make_async_remote_copy(
                src_ref=a, dst_ref=z, send_sem=ss.at[number, step], recv_sem=rs.at[number, step],
                device_id=where, device_id_type=MESH,
            )
            for a, z, step, where in made
        ]

    wargs = (wsend, wall, ws_sem, wr_sem)

    def everyone():
        made = []
        for az in range(ngz):
            for ay in range(ngy):
                for ax in range(ngx):
                    if ax + ay + az == 0:
                        continue
                    made.append(pltpu.make_async_remote_copy(
                        src_ref=bsend.at[:, pl.ds(0, 1)],
                        dst_ref=ball.at[X, core, :, pl.ds(row, 1)],
                        send_sem=bs_sem, recv_sem=br_sem,
                        device_id=((gx + ax) % ngx, (gy + ay) % ngy, (gz + az) % ngz),
                        device_id_type=MESH,
                    ))
        return made

    def start(number, args):
        for copy in stage(number, *args):
            copy.start()

    def finish(number, args):
        for copy in stage(number, *args):
            copy.wait_recv()

    v = [g_ref[e] for e in range(EQ)]
    send(0, v, nx, 1)
    for e in range(EQ):
        total = d_ref[e]
        for k in range(6):
            total = total + w_ref[6 * e + k]
        tot0[e] = total
        c0[e] = DAMP / total
        total = coarsen(d_ref[e], 1)
        wsend_d = coarsen(total, 2)
        for k in range(6):
            w = 0.25 * coarsen(w_ref[6 * e + k], 1)
            w1[6 * e + k] = w
            total = total + w
            wsend[6 * e + k] = to_rows((0.25 * coarsen(w, 2))[None])[0]
        wsend[6 * EQ + e] = to_rows(wsend_d[None])[0]
        tot1[e] = total
        c1[e] = DAMP / total
    own(wsend, wall, l_sem.at[0]).start()
    start(0, wargs)

    keep = 1.0 - DAMP

    def apply(r, v, n, s, weight, base, scale):
        ready = [
            before(v[e], e, n, s, weight, base(e), None if scale is None else scale[e])
            for e in range(EQ)
        ]
        if r != 5:
            receive(r, n, s)
        return [after(r, e, n, s, ready[e]) for e in range(EQ)]

    def smooth0(r, v):
        return apply(r, v, nx, 1, weight0, lambda e: keep * v[e] + c0[e] * b_ref[e], c0)

    def smooth1(r, v):
        return apply(r, v, nx // 2, 2, weight1, lambda e: keep * v[e] + c1[e] * b1[e], c1)

    v = smooth0(0, v)
    send(1, v, nx, 1)
    v = smooth0(1, v)
    own(wsend, wall, l_sem.at[0]).wait()
    finish(0, wargs)
    send(2, v, nx, 1)
    start(1, wargs)
    u = []
    rest = apply(2, v, nx, 1, weight0, lambda e: b_ref[e] - tot0[e] * v[e], None)
    for e in range(EQ):
        b = coarsen(rest[e], 1)
        b1[e] = b
        u.append(c1[e] * b)
    half = nx // 2
    send(3, u, half, 2)
    u = smooth1(3, u)
    finish(1, wargs)
    send(4, u, half, 2)
    start(2, wargs)
    rest = apply(4, u, half, 2, weight1, lambda e: b1[e] - tot1[e] * u[e], None)
    for e in range(EQ):
        bsend[e] = to_rows(coarsen(rest[e], 2)[None])[0]
    for copy in everyone():
        copy.start()
    own(bsend, ball, br_sem).start()
    finish(2, wargs)
    start(3, wargs)
    finish(3, wargs)

    shape = (ngz, rows, nz)
    r_i, l_i = iota(shape, 1), iota(shape, 2)
    g_i = iota(shape, 0)
    zi, yi, xi = l_i % qz, (l_i // qz) % qy, l_i // (qz * qy)
    gyi, gxi = r_i // ngx, r_i % ngx
    inside = [
        ~((xi == qx - 1) & (gxi == ngx - 1)), ~((xi == 0) & (gxi == 0)),
        ~((yi == qy - 1) & (gyi == ngy - 1)), ~((yi == 0) & (gyi == 0)),
        ~((zi == qz - 1) & (g_i == ngz - 1)), ~((zi == 0) & (g_i == 0)),
    ]

    def whole(ref, index):
        return ref[:, :, index].reshape(shape)

    def next_of(v):
        return jnp.concatenate([v[1:], v[:1]], axis=0)

    def prev_of(v):
        return jnp.concatenate([v[-1:], v[:-1]], axis=0)

    def near2(v):
        sy, sx = qz, qz * qy
        return [
            jnp.where(xi == qx - 1, roll(roll(v, (qx - 1) * sx, 2), -1, 1), roll(v, -sx, 2)),
            jnp.where(xi == 0, roll(roll(v, -(qx - 1) * sx, 2), 1, 1), roll(v, sx, 2)),
            jnp.where(yi == qy - 1, roll(roll(v, (qy - 1) * sy, 2), -ngx, 1), roll(v, -sy, 2)),
            jnp.where(yi == 0, roll(roll(v, -(qy - 1) * sy, 2), ngx, 1), roll(v, sy, 2)),
            jnp.where(zi == qz - 1, roll(next_of(v), qz - 1, 2), roll(v, -1, 2)),
            jnp.where(zi == 0, roll(prev_of(v), -(qz - 1), 2), roll(v, 1, 2)),
        ]

    def dot_near(weights, near):
        total = weights[0] * near[0]
        for k in range(1, 6):
            total = total + weights[k] * near[k]
        return total

    def pair(a):
        sy, sx = qz, qz * qy
        a = a + jnp.where(xi % 2 == 0, roll(a, -sx, 2), roll(a, sx, 2))
        a = a + jnp.where(yi % 2 == 0, roll(a, -sy, 2), roll(a, sy, 2))
        a = a + jnp.where(zi % 2 == 0, roll(a, -1, 2), roll(a, 1, 2))
        return a * 0.125

    groups = qx * qy
    tiles = ngz // groups
    shape3 = (tiles, rows, nz)
    r3, l3, t3 = iota(shape3, 1), iota(shape3, 2), iota(shape3, 0)
    inside3 = [
        r3 % ngx < ngx - 1, r3 % ngx > 0, r3 // ngx < ngy - 1, r3 // ngx > 0,
        ~((l3 >= nz - 2) & (t3 == tiles - 1)), ~((l3 < 2) & (t3 == 0)),
    ]

    def join(a):
        a = a.reshape(tiles, groups, rows, nz)
        got = a[:, 0]
        for j in range(1, groups):
            got = jnp.where(l3 // qz == j, a[:, j], got)
        return got

    def part(a):
        parts = []
        for j in range(groups):
            mine = jnp.where(l3 // qz == j, a, 0.0)
            size = qz
            while size < nz:
                mine = mine + roll(mine, size, 2)
                size *= 2
            parts.append(mine)
        return jnp.stack(parts, axis=1).reshape(shape)

    def near3(v):
        if tiles == 1:
            up, down = roll(v, -2, 2), roll(v, 2, 2)
        else:
            up = jnp.where(l3 >= nz - 2, roll(next_of(v), -2, 2), roll(v, -2, 2))
            down = jnp.where(l3 < 2, roll(prev_of(v), 2, 2), roll(v, 2, 2))
        return [roll(v, -1, 1), roll(v, 1, 1), roll(v, -ngx, 1), roll(v, ngx, 1), up, down]

    w2, t2, w3, t3s = [], [], [], []
    for e in range(EQ):
        plain = [whole(wall, 6 * e + k) for k in range(6)]
        d2 = whole(wall, 6 * EQ + e)
        total = d2
        for k in range(6):
            total = total + plain[k]
        t2.append(total)
        w2.append([jnp.where(inside[k], plain[k], 0.0) for k in range(6)])
        plain3 = [0.25 * join(pair(plain[k])) for k in range(6)]
        total = join(pair(d2))
        for k in range(6):
            total = total + plain3[k]
        t3s.append(total)
        w3.append([jnp.where(inside3[k], plain3[k], 0.0) for k in range(6)])
    c2 = [DAMP / t for t in t2]
    c3 = [DAMP / t for t in t3s]

    pltpu.make_async_copy(ball, ball, br_sem).wait()

    for e in range(EQ):
        rhs = whole(ball, e)
        v2 = c2[e] * rhs
        for step in range(SWEEPS - 1):
            v2 = keep * v2 + c2[e] * (rhs + dot_near(w2[e], near2(v2)))
        rest = rhs - t2[e] * v2 + dot_near(w2[e], near2(v2))
        rhs3 = join(pair(rest))
        v3 = c3[e] * rhs3
        for step in range(COARSE_SWEEPS - 1):
            v3 = keep * v3 + c3[e] * (rhs3 + dot_near(w3[e], near3(v3)))
        v2 = v2 + part(v3)
        for step in range(SWEEPS):
            v2 = keep * v2 + c2[e] * (rhs + dot_near(w2[e], near2(v2)))
        e2[e] = v2

    wide = groups * nz
    source = iota((nz, wide), 0)
    target = iota((nz, wide), 1)
    widen = jnp.where(source == (target // nz) * qz + (target % nz) // 4, 1.0, 0.0).astype(jnp.float32)
    around = [(gx, gy, gz, None)]
    for axis, index, count in ((0, gx, ngx), (1, gy, ngy), (2, gz, ngz)):
        for step in (-1, 1):
            at = [gx, gy, gz]
            at[axis] = jnp.clip(index + step, 0, count - 1)
            has = index > 0 if step < 0 else index < count - 1
            around.append((at[0], at[1], at[2], has))
    for e in range(EQ):
        for j, (ax, ay, az, has) in enumerate(around):
            line = e2[e, az, pl.ds(ay * ngx + ax, 1), :]
            if has is not None:
                line = jnp.where(has, line, 0.0)
            lines[e * 7 + j : e * 7 + j + 1, :] = line
    for j in range(EQ * 7, lines.shape[0]):
        lines[j : j + 1, :] = jnp.zeros((1, nz), jnp.float32)
    back = jnp.dot(lines[...], widen, precision=HIGH, preferred_element_type=jnp.float32)
    ysel = iota((ny, nz), 0) // 4

    def strip(e, j, x, y):
        col = (x * qy + y) * nz
        return jnp.broadcast_to(back[e * 7 + j : e * 7 + j + 1, col : col + nz], (ny, nz))

    def plane(e, j, x):
        got = strip(e, j, x, 0)
        for y in range(1, qy):
            got = jnp.where(ysel == y, strip(e, j, x, y), got)
        return got

    low, high = pack_r[4, 0], pack_r[4, 1]
    for e in range(EQ):
        halo_x[5, 0, e] = halo_x[4, 0, e] + plane(e, 1, qx - 1)
        halo_x[5, 1, e] = halo_x[4, 1, e] + plane(e, 2, 0)
        for x in range(qx):
            edge = jnp.where(ysel < qy // 2, strip(e, 3, x, qy - 1), strip(e, 4, x, 0))
            below, above = plane(e, 5, x), plane(e, 6, x)
            for i in (2 * x, 2 * x + 1):
                halo_y[5, e, i] = halo_y[4, e, i] + edge
                here = lane2 == e * half + i
                low = jnp.where(here, low + jnp.broadcast_to(below[:, nz - 1 : nz], (ny, nz)), low)
                high = jnp.where(here, high + jnp.broadcast_to(above[:, 0:1], (ny, nz)), high)
        u[e] = u[e] + spread(jnp.stack([plane(e, 0, x) for x in range(qx)]))
    pack_r[5, 0] = low
    pack_r[5, 1] = high
    u = smooth1(5, u)
    send(6, u, half, 2)
    u = smooth1(6, u)
    v = [field[2, e] + spread(u[e]) for e in range(EQ)]
    send(7, v, nx, 1)
    v = smooth0(7, v)
    send(8, v, nx, 1)
    v = smooth0(8, v)
    for e in range(EQ):
        out_ref[e] = v[e]

    for r in range(rounds):
        if r == 5:
            continue
        n, s = (half, 2) if 3 <= r <= 6 else (nx, 1)
        for copy, has_target, _, _ in copies(r, n, s):
            @pl.when(has_target)
            def _():
                copy.wait_send()
    for number in range(4):
        for copy in stage(number, *wargs):
            copy.wait_send()
    for copy in everyone():
        copy.wait_send()


def per_device(dims, cores, couplings, diagonal, right_side, guess):
    ngx, ngy, ngz = dims
    brick = guess.shape[1:]
    nx, ny, nz = brick
    half = nx // 2
    rows = ngx * ngy
    nX = ngz // cores
    rounds = 9
    peers = max(ngx, ngy, nX, cores)
    f32 = jnp.float32
    vmem = pltpu.VMEM
    dma = pltpu.SemaphoreType.DMA
    return pl.pallas_call(
        functools.partial(kernel, dims, cores),
        out_shape=jax.ShapeDtypeStruct(guess.shape, f32),
        in_specs=[pl.BlockSpec(memory_space=vmem)] * 4,
        out_specs=pl.BlockSpec(memory_space=vmem),
        scratch_shapes=[
            vmem((rounds, EQ) + brick, f32),
            vmem((rounds, 2, EQ, ny, nz), f32),
            vmem((rounds, EQ) + brick, f32),
            vmem((rounds, 2, ny, nz), f32),
            vmem((rounds, 2, ny, nz), f32),
            vmem((EQ,) + brick, f32),
            vmem((EQ,) + brick, f32),
            vmem((6 * EQ, half, ny, nz), f32),
            vmem((EQ, half, ny, nz), f32),
            vmem((EQ, half, ny, nz), f32),
            vmem((EQ, half, ny, nz), f32),
            vmem((7 * EQ, ny, nz), f32),
            vmem((nX, cores, 7 * EQ, rows, nz), f32),
            vmem((EQ, ny, nz), f32),
            vmem((nX, cores, EQ, rows, nz), f32),
            vmem((EQ, ngz, rows, nz), f32),
            vmem((-(-EQ * 7 // 8) * 8, nz), f32),
            dma((rounds, 6)),
            dma((rounds, 6)),
            dma((4, peers)),
            dma((4, peers)),
            dma,
            dma,
            dma((1,)),
        ],
        compiler_params=pltpu.CompilerParams(
            collective_id=0, has_side_effects=True, vmem_limit_bytes=60 * 1024 * 1024
        ),
    )(couplings, diagonal, right_side, guess)


def solution(mesh):
    dims = (mesh.shape["gx"], mesh.shape["gy"], mesh.shape["gz"])
    cores = 2 if dims[2] % 2 == 0 else 1
    spec = P(None, "gx", "gy", "gz")
    return jax.shard_map(
        functools.partial(per_device, dims, cores),
        mesh=mesh,
        in_specs=(spec,) * 4,
        out_specs=spec,
        check_vma=False,
    )
```

```python
import functools

import jax
import jax.numpy as jnp
from jax import lax
from jax.experimental import pallas as pl
from jax.experimental.pallas import tpu as pltpu
from jax.sharding import PartitionSpec as P

SWEEPS = 2
COARSE_SWEEPS = 8
DAMP = 0.8
EQ = 3
MESH = pl.DeviceIdType.MESH
HIGH = lax.Precision.HIGHEST


def roll(value, shift, axis):
    size = value.shape[axis]
    shift = shift % size
    return value if shift == 0 else pltpu.roll(value, shift, axis)


def iota(shape, axis):
    return lax.broadcasted_iota(jnp.int32, shape, axis)


def kernel(
    dims, cores, w_ref, d_ref, b_ref, g_ref, out_ref,
    field, halo_x, halo_y, pack_s, pack_r, tot0, c0, w1, tot1, c1, b1,
    wsend, wall, bsend, ball, e2, lines,
    s_sem, r_sem, ws_sem, wr_sem, bs_sem, br_sem, l_sem,
):
    ngx, ngy, ngz = dims
    nx, ny, nz = g_ref.shape[1:]
    qx, qy, qz = nx // 4, ny // 4, nz // 4
    rows = ngx * ngy
    nX = ngz // cores
    gx, gy, gz = lax.axis_index("gx"), lax.axis_index("gy"), lax.axis_index("gz")
    X, core = gz // cores, gz % cores
    row = gy * ngx + gx
    axes = (("gx", gx, ngx), ("gy", gy, ngy), ("gz", gz, ngz))

    def device(name, index):
        here = {"gx": gx, "gy": gy, "gz": gz}
        here[name] = index
        return (here["gx"], here["gy"], here["gz"])

    barrier = pltpu.get_barrier_semaphore()
    close = ngy <= 4 and ngz <= 4
    awaited = 0
    for name, index, count in axes:
        if close and name != "gx":
            for step in (-1, 1):
                @pl.when((index + step >= 0) & (index + step < count))
                def _():
                    pl.semaphore_signal(
                        barrier, inc=1, device_id=device(name, jnp.clip(index + step, 0, count - 1)),
                        device_id_type=MESH,
                    )
            awaited = awaited + (index > 0).astype(jnp.int32) + (index < count - 1).astype(jnp.int32)
        else:
            for step in range(1, count):
                pl.semaphore_signal(
                    barrier, inc=1, device_id=device(name, (index + step) % count), device_id_type=MESH
                )
            awaited = awaited + (count - 1)

    rounds = field.shape[0]
    for name, index, count in axes:
        for side in range(2):
            @pl.when(index == (0 if side == 0 else count - 1))
            def _():
                for r in range(rounds):
                    if name == "gx":
                        halo_x[r, side] = jnp.zeros(halo_x.shape[2:], jnp.float32)
                    elif name == "gy":
                        lo = 0 if side == 0 else ny // 2
                        halo_y[r, :, :, lo : lo + ny // 2] = jnp.zeros(
                            (EQ, nx, ny // 2, nz), jnp.float32
                        )
                    else:
                        pack_r[r, side] = jnp.zeros(pack_r.shape[2:], jnp.float32)

    pl.semaphore_wait(barrier, awaited)

    lane2 = iota((ny, nz), 1)

    def copies(r, n, s):
        src = g_ref if r == 0 else field.at[r]
        made = []
        for side in range(2):
            other = 1 - side
            for place, (name, index, count) in enumerate(axes):
                if name == "gx":
                    a = src.at[:, 0 if side == 0 else n - 1]
                    z = halo_x.at[r, other]
                elif name == "gy":
                    a = src.at[:, 0:n, pl.ds(0 if side == 0 else ny - s, s)]
                    z = halo_y.at[r, :, 0:n, pl.ds(ny - s if side == 0 else 0, s)]
                else:
                    a = pack_s.at[r, side]
                    z = pack_r.at[r, other]
                target = index - 1 if side == 0 else index + 1
                has_target = index > 0 if side == 0 else index < count - 1
                has_source = index < count - 1 if side == 0 else index > 0
                slot = 2 * place + side
                made.append((
                    pltpu.make_async_remote_copy(
                        src_ref=a, dst_ref=z,
                        send_sem=s_sem.at[r, slot], recv_sem=r_sem.at[r, slot],
                        device_id=device(name, jnp.clip(target, 0, count - 1)),
                        device_id_type=MESH,
                    ),
                    has_target, has_source, name,
                ))
        return made

    def send(r, value, n, s):
        made = copies(r, n, s)
        if r > 0:
            for e in range(EQ):
                field[r, e, 0:n] = value[e]
        for copy, has_target, _, name in made:
            if name != "gz":
                @pl.when(has_target)
                def _():
                    copy.start()
        low = jnp.zeros((ny, nz), jnp.float32)
        high = jnp.zeros((ny, nz), jnp.float32)
        for e in range(EQ):
            for i in range(n):
                here = lane2 == e * n + i
                low = jnp.where(here, jnp.broadcast_to(value[e][i, :, 0:1], (ny, nz)), low)
                high = jnp.where(here, jnp.broadcast_to(value[e][i, :, nz - 1 : nz], (ny, nz)), high)
        pack_s[r, 0] = low
        pack_s[r, 1] = high
        for copy, has_target, _, name in made:
            if name == "gz":
                @pl.when(has_target)
                def _():
                    copy.start()

    def receive(r, n, s):
        for copy, _, has_source, _ in copies(r, n, s):
            @pl.when(has_source)
            def _():
                copy.wait_recv()

    def before(v, e, n, s, weight, base, scale):
        shape = (n, ny, nz)
        y, z = iota(shape, 1), iota(shape, 2)
        edge = jnp.zeros((1, ny, nz), jnp.float32)
        near = [
            jnp.concatenate([v[1:], edge], axis=0),
            jnp.concatenate([edge, v[:-1]], axis=0),
            jnp.where(y >= ny - s, 0.0, roll(v, -s, 1)),
            jnp.where(y < s, 0.0, roll(v, s, 1)),
            jnp.where(z >= nz - s, 0.0, roll(v, -s, 2)),
            jnp.where(z < s, 0.0, roll(v, s, 2)),
        ]
        w = [weight(e, k) for k in range(6)]
        total = w[0] * near[0]
        for k in range(1, 6):
            total = total + w[k] * near[k]
        wy = jnp.where(y >= ny - s, w[2], jnp.where(y < s, w[3], 0.0))
        wz = jnp.where(z >= nz - s, w[4], jnp.where(z < s, w[5], 0.0))
        up, down = w[0][n - 1], w[1][0]
        if scale is not None:
            total, wy, wz = scale * total, scale * wy, scale * wz
            up, down = scale[n - 1] * up, scale[0] * down
        return base + total, up, down, wy, wz

    def after(r, e, n, s, ready):
        total, up, down, wy, wz = ready
        shape = (n, ny, nz)
        y, z = iota(shape, 1), iota(shape, 2)
        low = pack_r[r, 0]
        high = pack_r[r, 1]
        zl = jnp.stack([jnp.broadcast_to(low[:, e * n + i : e * n + i + 1], (ny, nz)) for i in range(n)])
        zh = jnp.stack([jnp.broadcast_to(high[:, e * n + i : e * n + i + 1], (ny, nz)) for i in range(n)])
        hy = jnp.where((y < s) | (y >= ny - s), halo_y[r, e, 0:n], 0.0)
        total = total + wy * hy + wz * jnp.where(z < s, zl, zh)
        first = total[0] + down * halo_x[r, 0, e]
        last = total[n - 1] + up * halo_x[r, 1, e]
        return jnp.concatenate([first[None], total[1 : n - 1], last[None]], axis=0)

    def coarsen(a, s):
        n = a.shape[0]
        a = jnp.stack([a[2 * i] + a[2 * i + 1] for i in range(n // 2)])
        y, z = iota(a.shape, 1), iota(a.shape, 2)
        a = a + jnp.where((y // s) % 2 == 0, roll(a, -s, 1), roll(a, s, 1))
        a = a + jnp.where((z // s) % 2 == 0, roll(a, -s, 2), roll(a, s, 2))
        return a * 0.125

    def spread(a):
        return jnp.stack([a[i // 2] for i in range(2 * a.shape[0])])

    def weight0(e, k):
        return w_ref[6 * e + k]

    def weight1(e, k):
        return w1[6 * e + k]

    source = iota((nz, nz), 0)
    target = iota((nz, nz), 1)
    squeeze = jnp.where(source == 4 * (target % qz), 1.0, 0.0).astype(jnp.float32)

    def to_rows(a):
        m = a.shape[0]
        c = jnp.dot(a.reshape(m * qx * ny, nz), squeeze, precision=HIGH,
                    preferred_element_type=jnp.float32).reshape(m, qx, ny, nz)
        shape = (m, ny, nz)
        lane = iota(shape, 2)
        got = jnp.zeros(shape, jnp.float32)
        for x in range(qx):
            for y in range(qy):
                part = roll(c[:, x], -4 * y, 1)
                got = jnp.where(lane // qz == x * qy + y, part, got)
        return got

    def own(small, whole, sem):
        return pltpu.make_async_copy(
            small.at[:, pl.ds(0, 1)], whole.at[X, core, :, pl.ds(row, 1)], sem
        )

    def stage(number, small, whole, ss, rs):
        made = []
        if number == 0:
            for step in range(1, ngx):
                made.append((small.at[:, pl.ds(0, 1)], whole.at[X, core, :, pl.ds(row, 1)],
                             step, device("gx", (gx + step) % ngx)))
        elif number == 1:
            block = whole.at[X, core, :, pl.ds(gy * ngx, ngx)]
            for step in range(1, ngy):
                made.append((block, block, step, device("gy", (gy + step) % ngy)))
        elif number == 2:
            block = whole.at[X, core]
            for step in range(1, nX):
                made.append((block, block, step, device("gz", ((X + step) % nX) * cores + core)))
        else:
            block = whole.at[:, core]
            for step in range(1, cores):
                made.append((block, block, step, device("gz", X * cores + (core + step) % cores)))
        return [
            pltpu.make_async_remote_copy(
                src_ref=a, dst_ref=z, send_sem=ss.at[number, step], recv_sem=rs.at[number, step],
                device_id=where, device_id_type=MESH,
            )
            for a, z, step, where in made
        ]

    wargs = (wsend, wall, ws_sem, wr_sem)

    def everyone():
        made = []
        for az in range(ngz):
            for ay in range(ngy):
                for ax in range(ngx):
                    if ax + ay + az == 0:
                        continue
                    made.append(pltpu.make_async_remote_copy(
                        src_ref=bsend.at[:, pl.ds(0, 1)],
                        dst_ref=ball.at[X, core, :, pl.ds(row, 1)],
                        send_sem=bs_sem, recv_sem=br_sem,
                        device_id=((gx + ax) % ngx, (gy + ay) % ngy, (gz + az) % ngz),
                        device_id_type=MESH,
                    ))
        return made

    def start(number, args):
        for copy in stage(number, *args):
            copy.start()

    def finish(number, args):
        for copy in stage(number, *args):
            copy.wait_recv()

    v = [g_ref[e] for e in range(EQ)]
    send(0, v, nx, 1)
    for e in range(EQ):
        total = d_ref[e]
        for k in range(6):
            total = total + w_ref[6 * e + k]
        tot0[e] = total
        c0[e] = DAMP / total
        total = coarsen(d_ref[e], 1)
        wsend_d = coarsen(total, 2)
        for k in range(6):
            w = 0.25 * coarsen(w_ref[6 * e + k], 1)
            w1[6 * e + k] = w
            total = total + w
            wsend[6 * e + k] = to_rows((0.25 * coarsen(w, 2))[None])[0]
        wsend[6 * EQ + e] = to_rows(wsend_d[None])[0]
        tot1[e] = total
        c1[e] = DAMP / total
    own(wsend, wall, l_sem.at[0]).start()
    start(0, wargs)

    keep = 1.0 - DAMP

    def apply(r, v, n, s, weight, base, scale):
        ready = [
            before(v[e], e, n, s, weight, base(e), None if scale is None else scale[e])
            for e in range(EQ)
        ]
        if r != 5:
            receive(r, n, s)
        return [after(r, e, n, s, ready[e]) for e in range(EQ)]

    def smooth0(r, v):
        return apply(r, v, nx, 1, weight0, lambda e: keep * v[e] + c0[e] * b_ref[e], c0)

    def smooth1(r, v):
        return apply(r, v, nx // 2, 2, weight1, lambda e: keep * v[e] + c1[e] * b1[e], c1)

    v = smooth0(0, v)
    send(1, v, nx, 1)
    v = smooth0(1, v)
    own(wsend, wall, l_sem.at[0]).wait()
    finish(0, wargs)
    send(2, v, nx, 1)
    start(1, wargs)
    u = []
    rest = apply(2, v, nx, 1, weight0, lambda e: b_ref[e] - tot0[e] * v[e], None)
    for e in range(EQ):
        b = coarsen(rest[e], 1)
        b1[e] = b
        u.append(c1[e] * b)
    half = nx // 2
    send(3, u, half, 2)
    u = smooth1(3, u)
    finish(1, wargs)
    send(4, u, half, 2)
    start(2, wargs)
    rest = apply(4, u, half, 2, weight1, lambda e: b1[e] - tot1[e] * u[e], None)
    bsend[...] = to_rows(jnp.stack([coarsen(rest[e], 2) for e in range(EQ)]))
    for copy in reversed(everyone()):
        copy.start()
    own(bsend, ball, br_sem).start()
    finish(2, wargs)
    start(3, wargs)
    finish(3, wargs)

    shape = (ngz, rows, nz)
    r_i, l_i = iota(shape, 1), iota(shape, 2)
    g_i = iota(shape, 0)
    zi, yi, xi = l_i % qz, (l_i // qz) % qy, l_i // (qz * qy)
    gyi, gxi = r_i // ngx, r_i % ngx
    inside = [
        ~((xi == qx - 1) & (gxi == ngx - 1)), ~((xi == 0) & (gxi == 0)),
        ~((yi == qy - 1) & (gyi == ngy - 1)), ~((yi == 0) & (gyi == 0)),
        ~((zi == qz - 1) & (g_i == ngz - 1)), ~((zi == 0) & (g_i == 0)),
    ]

    def whole(ref, index):
        return ref[:, :, index].reshape(shape)

    def next_of(v):
        return jnp.concatenate([v[1:], v[:1]], axis=0)

    def prev_of(v):
        return jnp.concatenate([v[-1:], v[:-1]], axis=0)

    def near2(v):
        sy, sx = qz, qz * qy
        return [
            jnp.where(xi == qx - 1, roll(roll(v, (qx - 1) * sx, 2), -1, 1), roll(v, -sx, 2)),
            jnp.where(xi == 0, roll(roll(v, -(qx - 1) * sx, 2), 1, 1), roll(v, sx, 2)),
            jnp.where(yi == qy - 1, roll(roll(v, (qy - 1) * sy, 2), -ngx, 1), roll(v, -sy, 2)),
            jnp.where(yi == 0, roll(roll(v, -(qy - 1) * sy, 2), ngx, 1), roll(v, sy, 2)),
            jnp.where(zi == qz - 1, roll(next_of(v), qz - 1, 2), roll(v, -1, 2)),
            jnp.where(zi == 0, roll(prev_of(v), -(qz - 1), 2), roll(v, 1, 2)),
        ]

    def dot_near(weights, near):
        total = weights[0] * near[0]
        for k in range(1, 6):
            total = total + weights[k] * near[k]
        return total

    def pair(a):
        sy, sx = qz, qz * qy
        a = a + jnp.where(xi % 2 == 0, roll(a, -sx, 2), roll(a, sx, 2))
        a = a + jnp.where(yi % 2 == 0, roll(a, -sy, 2), roll(a, sy, 2))
        a = a + jnp.where(zi % 2 == 0, roll(a, -1, 2), roll(a, 1, 2))
        return a * 0.125

    groups = qx * qy
    tiles = ngz // groups
    shape3 = (tiles, rows, nz)
    r3, l3, t3 = iota(shape3, 1), iota(shape3, 2), iota(shape3, 0)
    inside3 = [
        r3 % ngx < ngx - 1, r3 % ngx > 0, r3 // ngx < ngy - 1, r3 // ngx > 0,
        ~((l3 >= nz - 2) & (t3 == tiles - 1)), ~((l3 < 2) & (t3 == 0)),
    ]

    def join(a):
        a = a.reshape(tiles, groups, rows, nz)
        got = a[:, 0]
        for j in range(1, groups):
            got = jnp.where(l3 // qz == j, a[:, j], got)
        return got

    def part(a):
        parts = []
        for j in range(groups):
            mine = jnp.where(l3 // qz == j, a, 0.0)
            size = qz
            while size < nz:
                mine = mine + roll(mine, size, 2)
                size *= 2
            parts.append(mine)
        return jnp.stack(parts, axis=1).reshape(shape)

    def near3(v):
        if tiles == 1:
            up, down = roll(v, -2, 2), roll(v, 2, 2)
        else:
            up = jnp.where(l3 >= nz - 2, roll(next_of(v), -2, 2), roll(v, -2, 2))
            down = jnp.where(l3 < 2, roll(prev_of(v), 2, 2), roll(v, 2, 2))
        return [roll(v, -1, 1), roll(v, 1, 1), roll(v, -ngx, 1), roll(v, ngx, 1), up, down]

    w2, t2, w3, t3s = [], [], [], []
    for e in range(EQ):
        plain = [whole(wall, 6 * e + k) for k in range(6)]
        d2 = whole(wall, 6 * EQ + e)
        total = d2
        for k in range(6):
            total = total + plain[k]
        t2.append(total)
        w2.append([jnp.where(inside[k], plain[k], 0.0) for k in range(6)])
        plain3 = [0.25 * join(pair(plain[k])) for k in range(6)]
        total = join(pair(d2))
        for k in range(6):
            total = total + plain3[k]
        t3s.append(total)
        w3.append([jnp.where(inside3[k], plain3[k], 0.0) for k in range(6)])
    c2 = [DAMP / t for t in t2]
    c3 = [DAMP / t for t in t3s]

    pltpu.make_async_copy(ball, ball, br_sem).wait()

    every = range(EQ)
    rhs = [whole(ball, e) for e in every]

    def smooth2(v):
        return [keep * v[e] + c2[e] * (rhs[e] + dot_near(w2[e], near2(v[e]))) for e in every]

    v2 = [c2[e] * rhs[e] for e in every]
    for step in range(SWEEPS - 1):
        v2 = smooth2(v2)
    rest = [rhs[e] - t2[e] * v2[e] + dot_near(w2[e], near2(v2[e])) for e in every]
    rhs3 = [join(pair(rest[e])) for e in every]
    v3 = [c3[e] * rhs3[e] for e in every]
    for step in range(COARSE_SWEEPS - 1):
        v3 = [keep * v3[e] + c3[e] * (rhs3[e] + dot_near(w3[e], near3(v3[e]))) for e in every]
    v2 = [v2[e] + part(v3[e]) for e in every]
    for step in range(SWEEPS):
        v2 = smooth2(v2)
    for e in every:
        e2[e] = v2[e]

    wide = groups * nz
    source = iota((nz, wide), 0)
    target = iota((nz, wide), 1)
    widen = jnp.where(source == (target // nz) * qz + (target % nz) // 4, 1.0, 0.0).astype(jnp.float32)
    around = [(gx, gy, gz, None)]
    for axis, index, count in ((0, gx, ngx), (1, gy, ngy), (2, gz, ngz)):
        for step in (-1, 1):
            at = [gx, gy, gz]
            at[axis] = jnp.clip(index + step, 0, count - 1)
            has = index > 0 if step < 0 else index < count - 1
            around.append((at[0], at[1], at[2], has))
    for e in range(EQ):
        for j, (ax, ay, az, has) in enumerate(around):
            line = e2[e, az, pl.ds(ay * ngx + ax, 1), :]
            if has is not None:
                line = jnp.where(has, line, 0.0)
            lines[e * 7 + j : e * 7 + j + 1, :] = line
    for j in range(EQ * 7, lines.shape[0]):
        lines[j : j + 1, :] = jnp.zeros((1, nz), jnp.float32)
    back = jnp.dot(lines[...], widen, precision=HIGH, preferred_element_type=jnp.float32)
    ysel = iota((ny, nz), 0) // 4

    def strip(e, j, x, y):
        col = (x * qy + y) * nz
        return jnp.broadcast_to(back[e * 7 + j : e * 7 + j + 1, col : col + nz], (ny, nz))

    def plane(e, j, x):
        got = strip(e, j, x, 0)
        for y in range(1, qy):
            got = jnp.where(ysel == y, strip(e, j, x, y), got)
        return got

    low, high = pack_r[4, 0], pack_r[4, 1]
    for e in range(EQ):
        halo_x[5, 0, e] = halo_x[4, 0, e] + plane(e, 1, qx - 1)
        halo_x[5, 1, e] = halo_x[4, 1, e] + plane(e, 2, 0)
        for x in range(qx):
            edge = jnp.where(ysel < qy // 2, strip(e, 3, x, qy - 1), strip(e, 4, x, 0))
            below, above = plane(e, 5, x), plane(e, 6, x)
            for i in (2 * x, 2 * x + 1):
                halo_y[5, e, i] = halo_y[4, e, i] + edge
                here = lane2 == e * half + i
                low = jnp.where(here, low + jnp.broadcast_to(below[:, nz - 1 : nz], (ny, nz)), low)
                high = jnp.where(here, high + jnp.broadcast_to(above[:, 0:1], (ny, nz)), high)
        u[e] = u[e] + spread(jnp.stack([plane(e, 0, x) for x in range(qx)]))
    pack_r[5, 0] = low
    pack_r[5, 1] = high
    u = smooth1(5, u)
    send(6, u, half, 2)
    u = smooth1(6, u)
    v = [field[2, e] + spread(u[e]) for e in range(EQ)]
    send(7, v, nx, 1)
    v = smooth0(7, v)
    send(8, v, nx, 1)
    v = smooth0(8, v)
    for e in range(EQ):
        out_ref[e] = v[e]

    for r in range(rounds):
        if r == 5:
            continue
        n, s = (half, 2) if 3 <= r <= 6 else (nx, 1)
        for copy, has_target, _, _ in copies(r, n, s):
            @pl.when(has_target)
            def _():
                copy.wait_send()
    for number in range(4):
        for copy in stage(number, *wargs):
            copy.wait_send()
    for copy in everyone():
        copy.wait_send()


def per_device(dims, cores, couplings, diagonal, right_side, guess):
    ngx, ngy, ngz = dims
    brick = guess.shape[1:]
    nx, ny, nz = brick
    half = nx // 2
    rows = ngx * ngy
    nX = ngz // cores
    rounds = 9
    peers = max(ngx, ngy, nX, cores)
    f32 = jnp.float32
    vmem = pltpu.VMEM
    dma = pltpu.SemaphoreType.DMA
    return pl.pallas_call(
        functools.partial(kernel, dims, cores),
        out_shape=jax.ShapeDtypeStruct(guess.shape, f32),
        in_specs=[pl.BlockSpec(memory_space=vmem)] * 4,
        out_specs=pl.BlockSpec(memory_space=vmem),
        scratch_shapes=[
            vmem((rounds, EQ) + brick, f32),
            vmem((rounds, 2, EQ, ny, nz), f32),
            vmem((rounds, EQ) + brick, f32),
            vmem((rounds, 2, ny, nz), f32),
            vmem((rounds, 2, ny, nz), f32),
            vmem((EQ,) + brick, f32),
            vmem((EQ,) + brick, f32),
            vmem((6 * EQ, half, ny, nz), f32),
            vmem((EQ, half, ny, nz), f32),
            vmem((EQ, half, ny, nz), f32),
            vmem((EQ, half, ny, nz), f32),
            vmem((7 * EQ, ny, nz), f32),
            vmem((nX, cores, 7 * EQ, rows, nz), f32),
            vmem((EQ, ny, nz), f32),
            vmem((nX, cores, EQ, rows, nz), f32),
            vmem((EQ, ngz, rows, nz), f32),
            vmem((-(-EQ * 7 // 8) * 8, nz), f32),
            dma((rounds, 6)),
            dma((rounds, 6)),
            dma((4, peers)),
            dma((4, peers)),
            dma,
            dma,
            dma((1,)),
        ],
        compiler_params=pltpu.CompilerParams(
            collective_id=0, has_side_effects=True, vmem_limit_bytes=60 * 1024 * 1024
        ),
    )(couplings, diagonal, right_side, guess)


def solution(mesh):
    dims = (mesh.shape["gx"], mesh.shape["gy"], mesh.shape["gz"])
    cores = 2 if dims[2] % 2 == 0 else 1
    spec = P(None, "gx", "gy", "gz")
    return jax.shard_map(
        functools.partial(per_device, dims, cores),
        mesh=mesh,
        in_specs=(spec,) * 4,
        out_specs=spec,
        check_vma=False,
    )
```
